128 devices in a mesh: req: 8 (over x, core), mlp: 16 (over z, y).
Axes of the slice: x: 4, y: 4, z: 4, core: 2. Of those that a mesh axis runs over, the one named last changes fastest.
Arguments:
- residual_in: bfloat16 [16384, 1792], P(('req', 'mlp')), may hold values from -6 to 6
- query_in: bfloat16 [16384, 256], P(('req', 'mlp')), may hold values from -4 to 4
- key_in: bfloat16 [16384, 256], P(('req', 'mlp')), may hold values from -4 to 4
- values_in: bfloat16 [16384, 1792], P(('req', 'mlp')), may hold values from -6 to 6
- conv_weight: float32 [3, 1792], replicated, may hold values from -0.8 to 0.8
- prefix_state: float32 [8, 16, 273, 112], P('req', 'mlp'), may hold values from -896 to 896
- prefix_norm: float32 [8, 16, 273], P('req', 'mlp'), as said below
- prefix_owner: int32 [8], replicated, may hold values from 0 to 7, each once
- lengths: int32 [8, 4], P('req'), may hold values from 1 to 1024, 2048 in all within a row
- old_flags: int32 [8, 4], P('req'), may hold values 0 or 1
- out_weight: bfloat16 [1792, 1792], replicated, may hold values from -0.125 to 0.125
- mlp_gain: float32 [1792], replicated, may hold values from 0.5 to 1.5
- gate_weight: bfloat16 [1792, 4864], P(None, 'mlp'), may hold values from -0.125 to 0.125
- up_weight: bfloat16 [1792, 4864], P(None, 'mlp'), may hold values from -0.125 to 0.125
- down_weight: bfloat16 [4864, 1792], P('mlp'), may hold values from -0.078125 to 0.078125
- next_gain: float32 [1792], replicated, may hold values from 0.5 to 1.5
- qkv_weight: bfloat16 [1792, 2304], replicated, may hold values from -0.125 to 0.125
Outputs:
- hidden_out: bfloat16 [16384, 1792], P(('req', 'mlp'))
- next_qkv: bfloat16 [16384, 2304], P(('req', 'mlp'))
The draws below stay inside these ranges and needn't reach their ends.
Inputs may be any that keep to these rules, and one draw needn't show every extreme that they name: `prefix_owner`: each slot holds exactly one group's cached state. `lengths`: a group's requests follow one another in order and fill its 2048 tokens; the longest of a group has exactly half of 2048. `prefix_norm`: a head's cached normalizer is a sum of feature maps of earlier keys.
All inputs are finite; a program needn't handle non-finite values. No bound on the sum of `old_flags` on one device may be relied on, other than what follows from the above.
Results may differ from the reference program's by a relative error of at most 0.024.
Values may be sent and summed in bfloat16 or wider, within the bound.
A program may use at most 192 MiB of HBM per device.

```python
import math
import jax
import jax.numpy as jnp
import numpy as np
from jax import lax

D = 1792
H = 16
FD = 16
FF = 4864
CONV = 3
RQ = 4
HD = 112
FEAT = 273
QKV = 2304
SEQ = 2048
TOKENS = 16384
N_REQ = 8
N_MLP = 16


def draw_prefix_norm(key, part):
    key_points = jax.random.fold_in(key, 11)
    key_weights = jax.random.fold_in(key, 12)
    shape = (N_REQ, H, 32, FD)
    points = jax.random.normal(key_points, shape, jnp.float32)
    weights = jnp.exp(jax.random.uniform(key_weights, (N_REQ, H, 32), jnp.float32, math.log(4.0), math.log(64.0)))
    squares = (points[..., :, None] * points[..., None, :]).reshape(N_REQ, H, 32, FD * FD)
    constant = jnp.ones((N_REQ, H, 32, 1), jnp.float32)
    features = jnp.concatenate([constant, points * FD ** (-0.25), squares / (math.sqrt(2.0) * math.sqrt(FD))], axis=-1)
    return jnp.sum(weights[..., None] * features, axis=2)


def set_ends(result, key, low, largest):
    dims = result.shape
    spot = [jax.random.randint(jax.random.fold_in(key, axis), (), 0, dims[axis]) for axis in range(len(dims))]
    result = result.at[tuple(spot)].set(low)
    longest = dims.index(max(dims))
    spot[longest] = (spot[longest] + 1) % dims[longest]
    return result.at[tuple(spot)].set(largest)


def level_of(stream_key, dims, shards, least, top_value):
    level, own = 1.0, jax.random.fold_in(stream_key, 6)
    for dim, blocks in shards:
        steps = jnp.exp(jax.random.uniform(jax.random.fold_in(own, dim), (blocks,), jnp.float32, least / len(shards), top_value / len(shards)))
        level = level * jnp.repeat(steps, dims[dim] // blocks).reshape([-1 if axis == dim else 1 for axis in range(len(dims))])
    return level


def profile(count, total, bound, skew):
    loads = [(1 << 20) // math.isqrt(standing ** skew) + 1 for standing in range(2, count + 1)]
    rest, given = total - bound - (count - 1), [1] * (count - 1)
    while rest > 0:
        candidates = [i for i in range(count - 1) if given[i] < bound]
        pool, left = sum([loads[i] for i in candidates]), rest
        for i in candidates:
            more = min(bound - given[i], max(1, left * loads[i] // pool), rest)
            given[i] = given[i] + more
            rest = rest - more
    return np.array([bound] + given)


def ragged(key, number_of, total, bound, lean):
    if number_of == 2:
        one = jax.random.randint(key, (), max(1, total - bound), min(bound, total - 1) + 1)
        return jnp.stack([one, total - one])
    tallies = jnp.asarray(profile(number_of, total, bound, lean), jnp.int32)
    twos = (number_of - 1) // 2
    source_of, sink = tallies[1:1 + 2 * twos:2], tallies[2:2 + 2 * twos:2]
    room = jnp.minimum(source_of - 1, bound - sink)
    shifted = jax.random.randint(jax.random.fold_in(key, 1), (twos,), 0, 1 << 20) % (room + 1)
    tallies = tallies.at[1:1 + 2 * twos:2].set(source_of - shifted).at[2:2 + 2 * twos:2].set(sink + shifted)
    return tallies[jax.random.permutation(jax.random.fold_in(key, 2), number_of)]


def scatter_about(rng, shape, scale, bound, split=(), held_as=jnp.bfloat16):
    level = level_of(rng, shape, split, -0.22, 0.18) if split else 1.0
    values = jax.random.normal(rng, shape, jnp.float32) * scale * level
    return jnp.minimum(jnp.maximum(values, -bound), bound).astype(held_as)


def setup_inputs(seed: int = 0) -> dict:
    splits = jax.random.split(jax.random.key(seed), 18)
    residual_in = scatter_about(splits[0], (TOKENS, D), 1.0, 6.0, ((0, 128),))
    query_in = scatter_about(splits[1], (TOKENS, H * FD), 1.0, 4.0, ((0, 128),))
    key_in = scatter_about(splits[2], (TOKENS, H * FD), 1.0, 4.0, ((0, 128),))
    values_in = scatter_about(splits[3], (TOKENS, D), 1.0, 6.0, ((0, 128),))
    conv_weight = jnp.clip(jax.random.uniform(splits[4], (CONV, D), jnp.float32, -0.8, 0.8), -0.8, 0.8)
    prefix_state = scatter_about(splits[5], (N_REQ, H, FEAT, HD), 140.0, 896.0, ((0, 8), (1, 16)), jnp.float32)
    prefix_norm = draw_prefix_norm(jax.random.fold_in(splits[17], 71), 0)
    prefix_owner = jax.random.permutation(splits[7], N_REQ).astype(jnp.int32)
    lengths = jax.vmap(lambda own: ragged(own, RQ, SEQ, SEQ // 2, 2))(jax.random.split(splits[8], N_REQ)).reshape((N_REQ, RQ)).astype(jnp.int32)
    old_flags = set_ends((jax.random.randint(splits[9], (N_REQ, RQ), 0, 2) < 1).astype(jnp.int32), jax.random.fold_in(splits[9], 1), 0, 1)
    out_weight = scatter_about(splits[10], (D, D), D ** -0.5, 0.125)
    mlp_gain = jnp.clip(1.0 + 0.1 * jax.random.normal(splits[11], (D,), jnp.float32), 0.5, 1.5)
    gate_weight = scatter_about(splits[12], (D, FF), D ** -0.5, 0.125, ((1, 16),))
    up_weight = scatter_about(splits[13], (D, FF), D ** -0.5, 0.125, ((1, 16),))
    down_weight = scatter_about(splits[14], (FF, D), FF ** -0.5, 0.078125, ((0, 16),))
    next_gain = jnp.clip(1.0 + 0.1 * jax.random.normal(splits[15], (D,), jnp.float32), 0.5, 1.5)
    qkv_weight = scatter_about(splits[16], (D, QKV), D ** -0.5, 0.125)
    return {"residual_in": residual_in, "query_in": query_in, "key_in": key_in, "values_in": values_in, "conv_weight": conv_weight, "prefix_state": prefix_state, "prefix_norm": prefix_norm, "prefix_owner": prefix_owner, "lengths": lengths, "old_flags": old_flags, "out_weight": out_weight, "mlp_gain": mlp_gain, "gate_weight": gate_weight, "up_weight": up_weight, "down_weight": down_weight, "next_gain": next_gain, "qkv_weight": qkv_weight}


EPSILON = 1e-05
HIGHEST = lax.Precision.HIGHEST

def feature_map(entries):
    feat_dim = entries.shape[-1]
    leading = entries.shape[:-1]
    squares = (entries[..., :, None] * entries[..., None, :]).reshape(leading + (feat_dim * feat_dim,))
    constant = jnp.ones(leading + (1,), jnp.float32)
    return jnp.concatenate([constant, entries * feat_dim ** (-0.25), squares / (math.sqrt(2.0) * math.sqrt(feat_dim))], axis=-1)

def request_of(lengths, positions):
    boundary = jnp.cumsum(lengths).astype(jnp.int32)[:-1]
    which = lax.optimization_barrier(jnp.sum((positions[:, None] >= boundary[None, :]).astype(jnp.int32), axis=1)).astype(jnp.int32)
    return jnp.where(positions < 0, jnp.int32(-1), which).astype(jnp.int32)

def convolve(entries, weights, requests, earlier_rows, earlier_requests):
    tap_count = weights.shape[0]
    row_count = entries.shape[0]
    extended = jnp.concatenate([earlier_rows, entries], axis=0).astype(jnp.float32)
    request_rows = jnp.concatenate([earlier_requests, requests], axis=0)
    summed = jnp.zeros(entries.shape, jnp.float32)
    for shift_by in range(tap_count):
        first_row = tap_count - 1 - shift_by
        earlier = extended[first_row:first_row + row_count]
        matching = (request_rows[first_row:first_row + row_count] == requests)[:, None]
        summed = summed + weights[shift_by][None, :] * jnp.where(matching, earlier, 0.0)
    return summed.astype(jnp.bfloat16)

def block_output(feat_query, feat_key, entries, requests, before, token_flags, carry_state, carry_norm, prefix_state, prefix_norm):
    row_count = requests.shape[0]
    scores = jnp.einsum('bhf,chf->hbc', feat_query.astype(jnp.float32), feat_key.astype(jnp.float32), precision=HIGHEST)
    row_index = jnp.arange(row_count)
    visible = (row_index[:, None] >= row_index[None, :]) & (requests[:, None] == requests[None, :])
    scores = jnp.where(visible[None], scores, 0.0)
    normalizer = jnp.transpose(lax.optimization_barrier(jnp.sum(scores, axis=2)))
    numerator = jnp.einsum('hbc,che->bhe', scores.astype(jnp.bfloat16).astype(jnp.float32), entries.astype(jnp.float32), precision=HIGHEST)
    continues = (requests == before).astype(jnp.float32)
    query_wide = feat_query.astype(jnp.float32)
    numerator = numerator + token_flags[:, None, None] * jnp.einsum('bhf,hfe->bhe', query_wide, prefix_state, precision=HIGHEST)
    numerator = numerator + continues[:, None, None] * jnp.einsum('bhf,hfe->bhe', query_wide, carry_state, precision=HIGHEST)
    normalizer = normalizer + token_flags[:, None] * jnp.einsum('bhf,hf->bh', query_wide, prefix_norm, precision=HIGHEST)
    normalizer = normalizer + continues[:, None] * jnp.einsum('bhf,hf->bh', query_wide, carry_norm, precision=HIGHEST)
    return (numerator / normalizer[:, :, None]).astype(jnp.bfloat16)

def block_state(feat_key, entries, requests, before):
    in_last = (requests == requests[-1]).astype(jnp.float32)
    keys_last = feat_key.astype(jnp.float32) * in_last[:, None, None]
    state = jnp.einsum('bhf,bhe->hfe', keys_last, entries.astype(jnp.float32), precision=HIGHEST)
    norm_sum = lax.optimization_barrier(jnp.sum(keys_last, axis=0))
    started = (requests[-1] != before).astype(jnp.float32)
    return (state, norm_sum, started)

def run_blocks(query, key_rows, conv_values, requests, token_flags, prefix_state, prefix_norm, block_rows):
    total_rows, head_count, feat_dim = query.shape
    head_width = conv_values.shape[2]
    feat_total = 1 + feat_dim + feat_dim * feat_dim
    steps_count = total_rows // block_rows

    def advance(carried, inputs):
        carry_state, carry_norm, before = carried
        query_block, key_block, value_block, request_block, flag_block = inputs
        feat_query = feature_map(query_block.astype(jnp.float32)).astype(jnp.bfloat16)
        feat_key = feature_map(key_block.astype(jnp.float32)).astype(jnp.bfloat16)
        output = block_output(feat_query, feat_key, value_block, request_block, before, flag_block, carry_state, carry_norm, prefix_state, prefix_norm)
        state, norm_sum, started = block_state(feat_key, value_block, request_block, before)
        keeping = 1.0 - started
        return ((state + keeping * carry_state, norm_sum + keeping * carry_norm, request_block[-1]), output)
    initial = (jnp.zeros((head_count, feat_total, head_width), jnp.float32), jnp.zeros((head_count, feat_total), jnp.float32), jnp.array(-1, dtype=jnp.int32))
    inputs = (query.reshape(steps_count, block_rows, head_count, feat_dim), key_rows.reshape(steps_count, block_rows, head_count, feat_dim), conv_values.reshape(steps_count, block_rows, head_count, head_width), requests.reshape(steps_count, block_rows), token_flags.reshape(steps_count, block_rows))
    _, outputs = lax.scan(advance, initial, inputs)
    return outputs.reshape(total_rows, head_count, head_width)

def flag_lookup(requests, request_ids, flag_row):
    matches = requests[:, None] == request_ids[None, :]
    return lax.optimization_barrier(jnp.sum(jnp.where(matches, flag_row[None, :], 0.0), axis=1))

def rms_scale(entries, gain):
    return entries * lax.rsqrt(lax.optimization_barrier(jnp.mean(entries * entries, axis=-1, keepdims=True)) + EPSILON) * gain

def reference(residual_in, query_in, key_in, values_in, conv_weight, prefix_state, prefix_norm, prefix_owner, lengths, old_flags, out_weight, mlp_gain, gate_weight, up_weight, down_weight, next_gain, qkv_weight):
    shard_width = FF // N_MLP

    def one_group(group_id):
        first_row = (group_id * SEQ).astype(jnp.int32)
        residual = lax.dynamic_slice_in_dim(residual_in, first_row, SEQ, 0)
        query = lax.dynamic_slice_in_dim(query_in, first_row, SEQ, 0).reshape(SEQ, H, FD)
        key_rows = lax.dynamic_slice_in_dim(key_in, first_row, SEQ, 0).reshape(SEQ, H, FD)
        value_rows = lax.dynamic_slice_in_dim(values_in, first_row, SEQ, 0)
        positions = jnp.arange(SEQ, dtype=jnp.int32)
        requests = request_of(lengths[group_id], positions)
        conv_values = convolve(value_rows, conv_weight, requests, jnp.zeros((CONV - 1, D), jnp.bfloat16), jnp.full((CONV - 1,), -1, jnp.int32))
        token_flags = flag_lookup(requests, jnp.arange(RQ, dtype=jnp.int32), old_flags[group_id].astype(jnp.float32))
        owner_slot = prefix_owner[group_id]
        attended = run_blocks(query, key_rows, conv_values.reshape(SEQ, H, HD), requests, token_flags, prefix_state[owner_slot], prefix_norm[owner_slot], min(SEQ, 512))
        projected = jnp.dot(attended.reshape(SEQ, D), out_weight, preferred_element_type=jnp.float32)
        first_sum = (residual.astype(jnp.float32) + projected).astype(jnp.bfloat16)
        normed = rms_scale(first_sum.astype(jnp.float32), mlp_gain).astype(jnp.bfloat16)
        gate_rows = jnp.dot(normed, gate_weight, preferred_element_type=jnp.float32)
        up_rows = jnp.dot(normed, up_weight, preferred_element_type=jnp.float32)
        hidden = (jax.nn.silu(gate_rows) * up_rows).astype(jnp.bfloat16)

        def add_shard(summed, shard_id):
            offset = (shard_id * shard_width).astype(jnp.int32)
            partial_sum = jnp.dot(lax.dynamic_slice_in_dim(hidden, offset, shard_width, 1), lax.dynamic_slice_in_dim(down_weight, offset, shard_width, 0), preferred_element_type=jnp.float32)
            rounded = lax.optimization_barrier(partial_sum.astype(jnp.bfloat16)).astype(jnp.float32)
            return (summed + rounded, None)
        mlp_output, _ = lax.scan(add_shard, jnp.zeros((SEQ, D), jnp.float32), jnp.arange(N_MLP, dtype=jnp.int32))
        second_sum = (first_sum.astype(jnp.float32) + mlp_output).astype(jnp.bfloat16)
        normed_next = rms_scale(second_sum.astype(jnp.float32), next_gain).astype(jnp.bfloat16)
        projections = jnp.dot(normed_next, qkv_weight, preferred_element_type=jnp.float32).astype(jnp.bfloat16)
        return (second_sum, projections)
    second_sum, projections = lax.map(one_group, jnp.arange(N_REQ, dtype=jnp.int32))
    return (second_sum.reshape(TOKENS, D), projections.reshape(TOKENS, QKV))
```

```python
import functools

import jax
import jax.numpy as jnp
from jax import lax
from jax.experimental import pallas as pl
from jax.experimental.pallas import tpu as pltpu
from jax.sharding import PartitionSpec as P

EPSILON = 1e-05
MESH = pl.DeviceIdType.MESH
F32 = jnp.float32
BF16 = jnp.bfloat16

D = 1792
H = 16
FD = 16
HD = 112
SQ = FD * FD
ROWS = 128
SEQ = 2048
PACK = 2 * FD + HD
SROWS = 288
BLK = 256
NBLK = SEQ // BLK
SPAN = 5


def tdot(a, b):
    return lax.dot_general(a, b, (((0,), (0,)), ((), ())), preferred_element_type=F32)


def dot(a, b):
    return jnp.dot(a, b, preferred_element_type=F32)


def attention_kernel(
    lens, flags, owner, res, q_in, k_in, v_in, conv_w, pstate, pnorm, w_out, gain,
    first_out, normed_out,
    pack, got, states, keys, queries, values, feats, attn, att_in, w_buf,
    s_pack, r_pack, s_state, r_state, s_att, r_att, l_sem,
):
    g = lax.axis_index("req")
    m = lax.axis_index("mlp")
    n_req = lax.axis_size("req")
    n_mlp = lax.axis_size("mlp")

    barrier = pltpu.get_barrier_semaphore()
    for d in range(1, n_mlp):
        pl.semaphore_signal(
            barrier, inc=1, device_id={"mlp": lax.rem(m + d, n_mlp)}, device_id_type=MESH
        )
    for d in range(1, n_req):
        pl.semaphore_signal(
            barrier, inc=1, device_id={"req": lax.rem(g + d, n_req)}, device_id_type=MESH
        )
    w_copy = pltpu.make_async_copy(w_out, w_buf, l_sem.at[0])
    w_copy.start()

    pack[:, 0:FD, :] = (q_in[...].T).reshape(H, FD, ROWS)
    pack[:, FD : 2 * FD, :] = (k_in[...].T).reshape(H, FD, ROWS)
    pack[:, 2 * FD :, :] = (v_in[...].T).reshape(H, HD, ROWS)

    eye = (
        lax.broadcasted_iota(jnp.int32, (1 + FD + SQ, 1 + FD + SQ), 0)
        == lax.broadcasted_iota(jnp.int32, (1 + FD + SQ, 1 + FD + SQ), 1)
    )
    norm_col = jnp.sum(jnp.where(eye, pnorm[...], 0.0), axis=1, keepdims=True)
    norm_hi = norm_col.astype(BF16).astype(F32)
    full = jnp.concatenate(
        [
            pstate[...],
            norm_hi,
            norm_col - norm_hi,
            jnp.zeros((1 + FD + SQ, ROWS - HD - 2), F32),
        ],
        axis=1,
    )
    states[g] = jnp.concatenate(
        [
            full[1 + FD :],
            full[1 : 1 + FD],
            full[0:1],
            jnp.zeros((SROWS - 1 - FD - SQ, ROWS), F32),
        ],
        axis=0,
    ).astype(BF16)

    pl.semaphore_wait(barrier, n_mlp - 1 + n_req - 1)

    def pack_copy(to, frm):
        return pltpu.make_async_remote_copy(
            src_ref=pack.at[to], dst_ref=got.at[frm], send_sem=s_pack.at[to], recv_sem=r_pack.at[frm],
            device_id={"mlp": to}, device_id_type=MESH,
        )

    def state_copy(to, frm):
        return pltpu.make_async_remote_copy(
            src_ref=states.at[g], dst_ref=states.at[frm], send_sem=s_state.at[to], recv_sem=r_state.at[frm],
            device_id={"req": to}, device_id_type=MESH,
        )

    for d in range(1, n_mlp):
        pack_copy(lax.rem(m + d, n_mlp), m).start()
    for d in range(1, n_req):
        state_copy(lax.rem(g + d, n_req), g).start()
    got[m] = pack[m]

    b0 = lens[0, 0]
    b1 = b0 + lens[0, 1]
    b2 = b1 + lens[0, 2]
    f0, f1, f2, f3 = (flags[0, i].astype(F32) for i in range(4))

    def starts(pos):
        return jnp.where(pos >= b2, b2, jnp.where(pos >= b1, b1, jnp.where(pos >= b0, b0, 0)))

    for d in range(1, n_mlp):
        pack_copy(m, lax.rem(m + d, n_mlp)).wait_recv()
    for j in range(H):
        queries[:, j * ROWS : (j + 1) * ROWS] = got[j, 0:FD, :]
        keys[j * ROWS : (j + 1) * ROWS, :] = got[j, FD : 2 * FD, :].T
    raw = jnp.concatenate([got[j, 2 * FD :, :] for j in range(H)], axis=1).astype(F32)
    pos = lax.broadcasted_iota(jnp.int32, (1, SEQ), 1)
    start = starts(pos)
    conv = conv_w[0, m] * raw
    for tap in (1, 2):
        conv = conv + conv_w[tap, m] * jnp.where(pos - tap >= start, pltpu.roll(raw, tap, 1), 0.0)
    values[...] = conv.astype(BF16)

    old = jnp.where(pos >= b2, f3, jnp.where(pos >= b1, f2, jnp.where(pos >= b0, f1, f0)))
    qf = queries[...].astype(F32)
    for a in range(FD):
        feats[a * FD : (a + 1) * FD, :] = (
            old * (qf[a : a + 1] * qf * (1.0 / 32.0**0.5))
        ).astype(BF16)
    feats[SQ : SQ + FD, :] = (old * (0.5 * qf)).astype(BF16)
    feats[SQ + FD :, :] = jnp.concatenate([old, jnp.zeros((SROWS - SQ - FD - 1, SEQ), F32)], axis=0).astype(BF16)

    for d in range(1, n_req):
        state_copy(g, lax.rem(g + d, n_req)).wait_recv()
    own_state = states[owner[g]]

    def att_copy(to, frm):
        return pltpu.make_async_remote_copy(
            src_ref=attn.at[to], dst_ref=att_in.at[frm], send_sem=s_att.at[to], recv_sem=r_att.at[frm],
            device_id={"mlp": to}, device_id_type=MESH,
        )

    def query_block(i, _):
        at = pl.multiple_of(i * BLK, BLK)
        q_blk = queries[:, pl.ds(at, BLK)]
        old_part = tdot(own_state, feats[:, pl.ds(at, BLK)])
        q_pos = at + lax.broadcasted_iota(jnp.int32, (1, BLK), 1)
        q_start = starts(q_pos)
        q_scaled = (q_blk.astype(F32) * 0.25).astype(BF16)

        def key_block(j, carry):
            num, den = carry
            k_at = pl.multiple_of(j * BLK, BLK)
            t = dot(keys[pl.ds(k_at, BLK), :], q_scaled) + 1.0
            p = t * t * 0.5 + 0.5
            k_pos = k_at + lax.broadcasted_iota(jnp.int32, (BLK, 1), 0)
            p = jnp.where((k_pos >= q_start) & (k_pos <= q_pos), p, 0.0)
            den = den + jnp.sum(p, axis=0, keepdims=True)
            num = num + dot(values[:, pl.ds(k_at, BLK)], p.astype(BF16))
            return num, den

        num, den = lax.fori_loop(
            jnp.maximum(i - (SPAN - 1), 0),
            i + 1,
            key_block,
            (old_part[:HD], old_part[HD : HD + 1] + old_part[HD + 1 : HD + 2]),
        )
        out = (num / den).astype(BF16)
        for half in range(BLK // ROWS):
            to = i * (BLK // ROWS) + half
            attn[to] = out[:, half * ROWS : (half + 1) * ROWS]

            @pl.when(to != m)
            def _():
                att_copy(to, m).start()

            @pl.when(to == m)
            def _():
                att_in[m] = out[:, half * ROWS : (half + 1) * ROWS]

        return 0

    lax.fori_loop(0, NBLK, query_block, 0)

    for d in range(1, n_mlp):
        pack_copy(lax.rem(m + d, n_mlp), m).wait_send()
    for d in range(1, n_req):
        state_copy(lax.rem(g + d, n_req), g).wait_send()
    w_copy.wait()
    for d in range(1, n_mlp):
        att_copy(m, lax.rem(m + d, n_mlp)).wait_recv()
    attended = att_in[...].reshape(D, ROWS).T
    first = (res[...].astype(F32) + dot(attended, w_buf[...])).astype(BF16)
    first_out[...] = first
    wide = first.astype(F32)
    normed_out[...] = (
        wide * lax.rsqrt(jnp.mean(wide * wide, axis=-1, keepdims=True) + EPSILON) * gain[...]
    ).astype(BF16)
    for d in range(1, n_mlp):
        att_copy(lax.rem(m + d, n_mlp), m).wait_send()


def attention(lengths, old_flags, owner, res, q, k, v, conv_w, pstate, pnorm, w_out, gain):
    smem = pl.BlockSpec(memory_space=pltpu.SMEM)
    vmem = pl.BlockSpec(memory_space=pltpu.VMEM)
    return pl.pallas_call(
        attention_kernel,
        out_shape=(jax.ShapeDtypeStruct((ROWS, D), BF16), jax.ShapeDtypeStruct((ROWS, D), BF16)),
        in_specs=[smem] * 3 + [vmem] * 7 + [pl.BlockSpec(memory_space=pl.ANY), vmem],
        out_specs=(vmem, vmem),
        scratch_shapes=[
            pltpu.VMEM((H, PACK, ROWS), BF16),
            pltpu.VMEM((H, PACK, ROWS), BF16),
            pltpu.VMEM((8, SROWS, ROWS), BF16),
            pltpu.VMEM((SEQ, FD), BF16),
            pltpu.VMEM((FD, SEQ), BF16),
            pltpu.VMEM((HD, SEQ), BF16),
            pltpu.VMEM((SROWS, SEQ), BF16),
            pltpu.VMEM((H, HD, ROWS), BF16),
            pltpu.VMEM((H, HD, ROWS), BF16),
            pltpu.VMEM((D, D), BF16),
            pltpu.SemaphoreType.DMA((H,)),
            pltpu.SemaphoreType.DMA((H,)),
            pltpu.SemaphoreType.DMA((8,)),
            pltpu.SemaphoreType.DMA((8,)),
            pltpu.SemaphoreType.DMA((H,)),
            pltpu.SemaphoreType.DMA((H,)),
            pltpu.SemaphoreType.DMA((1,)),
        ],
        compiler_params=pltpu.CompilerParams(
            collective_id=0, has_side_effects=True, vmem_limit_bytes=56 << 20
        ),
        name="attention",
    )(lengths, old_flags, owner, res, q, k, v, conv_w, pstate, pnorm, w_out, gain)


def rms_scale(entries, gain):
    return entries * lax.rsqrt(jnp.mean(entries * entries, axis=-1, keepdims=True) + EPSILON) * gain


def shards(
    residual_in, query_in, key_in, values_in, conv_weight, prefix_state, prefix_norm, prefix_owner,
    lengths, old_flags, out_weight, mlp_gain, gate_weight, up_weight, down_weight, next_gain, qkv_weight,
):
    first_sum, normed = attention(
        lengths, old_flags, prefix_owner, residual_in, query_in, key_in, values_in,
        conv_weight.reshape(3, H, HD, 1), prefix_state.reshape(1 + FD + SQ, HD),
        prefix_norm.reshape(1, 1 + FD + SQ), out_weight, mlp_gain.reshape(1, D),
    )
    row_piece = lax.all_gather(normed, "mlp", axis=0, tiled=True)
    gate_rows = jnp.dot(row_piece, gate_weight, preferred_element_type=F32)
    up_rows = jnp.dot(row_piece, up_weight, preferred_element_type=F32)
    hidden = (jax.nn.silu(gate_rows) * up_rows).astype(BF16)
    mlp_output = lax.psum_scatter(
        jnp.dot(hidden, down_weight, preferred_element_type=F32).astype(BF16),
        "mlp", scatter_dimension=0, tiled=True,
    ).astype(F32)
    second_sum = (first_sum.astype(F32) + mlp_output).astype(BF16)
    normed_next = rms_scale(second_sum.astype(F32), next_gain).astype(BF16)
    projections = jnp.dot(normed_next, qkv_weight, preferred_element_type=F32).astype(BF16)
    return (second_sum, projections)


def solution(mesh):
    placed = (
        P(("req", "mlp"), None), P(("req", "mlp"), None), P(("req", "mlp"), None), P(("req", "mlp"), None),
        P(), P("req", "mlp", None, None), P("req", "mlp", None), P(), P("req", None), P("req", None),
        P(), P(), P(None, "mlp"), P(None, "mlp"), P("mlp", None), P(), P(),
    )
    return jax.shard_map(
        shards,
        mesh=mesh,
        in_specs=placed,
        out_specs=(P(("req", "mlp"), None), P(("req", "mlp"), None)),
        check_vma=False,
    )
```

```python
import functools

import jax
import jax.numpy as jnp
from jax import lax
from jax.experimental import pallas as pl
from jax.experimental.pallas import tpu as pltpu
from jax.sharding import PartitionSpec as P

EPSILON = 1e-05
MESH = pl.DeviceIdType.MESH
F32 = jnp.float32
BF16 = jnp.bfloat16

D = 1792
H = 16
FD = 16
HD = 112
SQ = FD * FD
ROWS = 128
SEQ = 2048
PACK = 2 * FD + HD
SROWS = 288
BLK = 256
NBLK = SEQ // BLK
SPAN = 5
QKV = 2304
HID = 304
LANES = D // 2
XROWS = 48
ZROW = 4 * XROWS
ZMID = 256
XMID = 512
HALF = ROWS // 2
CHUNK = 256
EARLY_Z = True


def tdot(a, b):
    return lax.dot_general(a, b, (((0,), (0,)), ((), ())), preferred_element_type=F32)


def dot(a, b):
    return jnp.dot(a, b, preferred_element_type=F32)


def dot_t(a, b):
    return lax.dot_general(a, b, (((1,), (1,)), ((), ())), preferred_element_type=F32)


def rms_scale(wide, gain):
    return (wide * lax.rsqrt(jnp.mean(wide * wide, axis=-1, keepdims=True) + EPSILON) * gain).astype(BF16)


def layer_kernel(
    lens, flags, owner, res, q_in, k_in, v_in, conv_w, pstate, pnorm, w_out, gain,
    w_gate, w_up, w_down, next_gain, w_qkv,
    hidden_out, qkv_out,
    pack, got, states, keys, queries, values, feats, attn, att_in, w_buf, taps, state_in,
    ffn, qkv_buf, rows, part, via, back,
    s_pack, r_pack, s_state, r_state, s_att, r_att, l_sem, s_w, r_w, s_rows, r_rows, s_part, r_part,
):
    g = lax.axis_index("req")
    m = lax.axis_index("mlp")
    n_req = lax.axis_size("req")
    n_mlp = lax.axis_size("mlp")
    x, core = g // 2, lax.rem(g, 2)
    z, y = m // 4, lax.rem(m, 4)

    barrier = pltpu.get_barrier_semaphore()
    for d in range(1, n_mlp):
        pl.semaphore_signal(
            barrier, inc=1, device_id={"mlp": lax.rem(m + d, n_mlp)}, device_id_type=MESH
        )
    for d in range(1, n_req):
        pl.semaphore_signal(
            barrier, inc=1, device_id={"req": lax.rem(g + d, n_req)}, device_id_type=MESH
        )
    state_load = pltpu.make_async_copy(pstate.at[:, 0, :], state_in, l_sem.at[0])
    state_load.start()
    ffn_loads = [
        pltpu.make_async_copy(ref, ffn.at[i, 0], l_sem.at[1 + i])
        for i, ref in enumerate((w_gate, w_up, w_down))
    ]
    for load in ffn_loads:
        load.start()
    w_copy = pltpu.make_async_copy(w_out, w_buf, l_sem.at[4])
    w_copy.start()
    qkv_copy = pltpu.make_async_copy(w_qkv, qkv_buf, l_sem.at[5])
    qkv_copy.start()

    lane0 = pl.multiple_of(core * LANES, 128)

    def weights_to(k, axis, to, slots, slots_there, row0, count, lane_at=0, lane_count=LANES):
        lanes = pl.ds(pl.multiple_of(lane0 + lane_at, 128), lane_count)
        at = pl.ds(row0, count)
        return pltpu.make_async_remote_copy(
            src_ref=ffn.at[:, slots, at, lanes], dst_ref=ffn.at[:, slots_there, at, lanes],
            send_sem=s_w.at[k], recv_sem=r_w.at[k], device_id={axis: to}, device_id_type=MESH,
        )

    def z_at(step):
        return lax.rem(z + step + 4, 4) * 4 + y

    def x_at(step):
        return lax.rem(x + step + 4, 4) * 2 + core

    def y_at(step):
        return z * 4 + lax.rem(y + step + 4, 4)

    sibling = x * 2 + 1 - core
    away = pl.ds(1, 3)
    mine = pl.multiple_of(x * XROWS, 16)
    left_rows = pl.multiple_of(lax.rem(x + 3, 4) * XROWS, 16)
    right_rows = pl.multiple_of(lax.rem(x + 1, 4) * XROWS, 16)
    far_rows = pl.multiple_of(lax.rem(x + 2, 4) * XROWS, 16)
    one, two, three = pl.ds(1, 1), pl.ds(2, 1), pl.ds(3, 1)
    own = pl.ds(0, 1)
    z_quarter = [
        weights_to(0, "mlp", z_at(1), own, one, mine, XROWS),
        weights_to(1, "mlp", z_at(-1), own, two, mine, XROWS),
        weights_to(2, "mlp", z_at(2), own, three, mine, XROWS),
    ]
    z_rest = [
        weights_to(3, "mlp", z_at(1), own, one, ZROW, HID - ZROW),
        weights_to(4, "mlp", z_at(-1), own, two, ZROW, HID - ZROW),
    ]
    z_far = [
        weights_to(5, "mlp", z_at(1), one, three, ZROW, ZMID - ZROW),
        weights_to(6, "mlp", z_at(-1), two, three, ZMID, HID - ZMID),
    ]
    x_next = [
        weights_to(7, "req", x_at(1), away, away, mine, XROWS),
        weights_to(8, "req", x_at(-1), away, away, mine, XROWS),
    ]
    x_next_in = [
        weights_to(7, "req", x_at(1), away, away, left_rows, XROWS),
        weights_to(8, "req", x_at(-1), away, away, right_rows, XROWS),
    ]
    x_far = [
        weights_to(9, "req", x_at(1), away, away, left_rows, XROWS, 0, XMID),
        weights_to(10, "req", x_at(-1), away, away, right_rows, XROWS, XMID, LANES - XMID),
    ]
    pair = [
        weights_to(11, "req", sibling, away, away, mine, XROWS),
        weights_to(12, "req", sibling, away, away, left_rows, XROWS),
        weights_to(13, "req", sibling, away, away, right_rows, XROWS),
        weights_to(14, "req", sibling, away, away, far_rows, XROWS, 0, XMID),
        weights_to(15, "req", sibling, away, away, far_rows, XROWS, XMID, LANES - XMID),
        weights_to(16, "req", sibling, one, one, ZROW, HID - ZROW),
        weights_to(17, "req", sibling, two, two, ZROW, HID - ZROW),
        weights_to(18, "req", sibling, three, three, ZROW, ZMID - ZROW),
        weights_to(19, "req", sibling, three, three, ZMID, HID - ZMID),
    ]

    pack[:, 0:FD, :] = (q_in[...].T).reshape(H, FD, ROWS)
    pack[:, FD : 2 * FD, :] = (k_in[...].T).reshape(H, FD, ROWS)
    pack[:, 2 * FD :, :] = (v_in[...].T).reshape(H, HD, ROWS)

    eye = (
        lax.broadcasted_iota(jnp.int32, (1 + FD + SQ, 1 + FD + SQ), 0)
        == lax.broadcasted_iota(jnp.int32, (1 + FD + SQ, 1 + FD + SQ), 1)
    )
    norm_col = jnp.sum(jnp.where(eye, pnorm[...], 0.0), axis=1, keepdims=True)
    norm_hi = norm_col.astype(BF16).astype(F32)
    state_load.wait()
    full = jnp.concatenate(
        [
            state_in[...],
            norm_hi,
            norm_col - norm_hi,
            jnp.zeros((1 + FD + SQ, ROWS - HD - 2), F32),
        ],
        axis=1,
    )
    states[g] = jnp.concatenate(
        [
            full[1 + FD :],
            full[1 : 1 + FD],
            full[0:1],
            jnp.zeros((SROWS - 1 - FD - SQ, ROWS), F32),
        ],
        axis=0,
    ).astype(BF16)

    taps[...] = (
        jnp.concatenate([conv_w[...], jnp.zeros((5, D), F32)], axis=0).T
    ).reshape(H, HD, 8)

    pl.semaphore_wait(barrier, n_mlp - 1 + n_req - 1)

    def pack_copy(to, frm):
        return pltpu.make_async_remote_copy(
            src_ref=pack.at[to], dst_ref=got.at[frm], send_sem=s_pack.at[to], recv_sem=r_pack.at[frm],
            device_id={"mlp": to}, device_id_type=MESH,
        )

    def state_copy(to, frm):
        return pltpu.make_async_remote_copy(
            src_ref=states.at[g], dst_ref=states.at[frm], send_sem=s_state.at[to], recv_sem=r_state.at[frm],
            device_id={"req": to}, device_id_type=MESH,
        )

    for d in range(1, n_mlp):
        pack_copy(lax.rem(m + d, n_mlp), m).start()
    for d in range(1, n_req):
        state_copy(lax.rem(g + d, n_req), g).start()
    got[m] = pack[m]
    for load in ffn_loads:
        load.wait()
    for copy in z_quarter:
        copy.start()
    if EARLY_Z:
        for copy in z_rest:
            copy.start()

    b0 = lens[0, 0]
    b1 = b0 + lens[0, 1]
    b2 = b1 + lens[0, 2]
    f0, f1, f2, f3 = (flags[0, i].astype(F32) for i in range(4))

    def starts(pos):
        return jnp.where(pos >= b2, b2, jnp.where(pos >= b1, b1, jnp.where(pos >= b0, b0, 0)))

    for d in range(1, n_mlp):
        pack_copy(m, lax.rem(m + d, n_mlp)).wait_recv()
    for j in range(H):
        queries[:, j * ROWS : (j + 1) * ROWS] = got[j, 0:FD, :]
        keys[j * ROWS : (j + 1) * ROWS, :] = got[j, FD : 2 * FD, :].T
    raw = jnp.concatenate([got[j, 2 * FD :, :] for j in range(H)], axis=1).astype(F32)
    pos = lax.broadcasted_iota(jnp.int32, (1, SEQ), 1)
    start = starts(pos)
    tap_cols = taps[m]
    conv = tap_cols[:, 0:1] * raw
    for tap in (1, 2):
        conv = conv + tap_cols[:, tap : tap + 1] * jnp.where(pos - tap >= start, pltpu.roll(raw, tap, 1), 0.0)
    values[...] = conv.astype(BF16)

    old = jnp.where(pos >= b2, f3, jnp.where(pos >= b1, f2, jnp.where(pos >= b0, f1, f0)))
    qf = queries[...].astype(F32)
    for a in range(FD):
        feats[a * FD : (a + 1) * FD, :] = (
            old * (qf[a : a + 1] * qf * (1.0 / 32.0**0.5))
        ).astype(BF16)
    feats[SQ : SQ + FD, :] = (old * (0.5 * qf)).astype(BF16)
    feats[SQ + FD :, :] = jnp.concatenate([old, jnp.zeros((SROWS - SQ - FD - 1, SEQ), F32)], axis=0).astype(BF16)

    for d in range(1, n_req):
        state_copy(g, lax.rem(g + d, n_req)).wait_recv()
    own_state = states[owner[g]]

    def att_copy(to, frm):
        return pltpu.make_async_remote_copy(
            src_ref=attn.at[to], dst_ref=att_in.at[frm], send_sem=s_att.at[to], recv_sem=r_att.at[frm],
            device_id={"mlp": to}, device_id_type=MESH,
        )

    def query_block(i, _):
        at = pl.multiple_of(i * BLK, BLK)
        q_blk = queries[:, pl.ds(at, BLK)]
        old_part = tdot(own_state, feats[:, pl.ds(at, BLK)])
        q_pos = at + lax.broadcasted_iota(jnp.int32, (1, BLK), 1)
        q_start = starts(q_pos)
        q_scaled = (q_blk.astype(F32) * 0.25).astype(BF16)

        def key_block(j, carry):
            num, den = carry
            k_at = pl.multiple_of(j * BLK, BLK)
            t = dot(keys[pl.ds(k_at, BLK), :], q_scaled) + 1.0
            p = t * t * 0.5 + 0.5
            k_pos = k_at + lax.broadcasted_iota(jnp.int32, (BLK, 1), 0)
            p = jnp.where((k_pos >= q_start) & (k_pos <= q_pos), p, 0.0)
            den = den + jnp.sum(p, axis=0, keepdims=True)
            num = num + dot(values[:, pl.ds(k_at, BLK)], p.astype(BF16))
            return num, den

        num, den = lax.fori_loop(
            jnp.maximum(i - (SPAN - 1), 0),
            i + 1,
            key_block,
            (old_part[:HD], old_part[HD : HD + 1] + old_part[HD + 1 : HD + 2]),
        )
        out = (num / den).astype(BF16)
        for half in range(BLK // ROWS):
            to = i * (BLK // ROWS) + half
            attn[to] = out[:, half * ROWS : (half + 1) * ROWS]

            @pl.when(to != m)
            def _():
                att_copy(to, m).start()

            @pl.when(to == m)
            def _():
                att_in[m] = out[:, half * ROWS : (half + 1) * ROWS]

        return 0

    lax.fori_loop(0, NBLK, query_block, 0)

    if not EARLY_Z:
        for copy in z_rest:
            copy.start()
    for copy in z_quarter:
        copy.wait_recv()
    for copy in x_next:
        copy.start()
    pair[0].start()

    for d in range(1, n_mlp):
        pack_copy(lax.rem(m + d, n_mlp), m).wait_send()
    for d in range(1, n_req):
        state_copy(lax.rem(g + d, n_req), g).wait_send()
    w_copy.wait()
    for d in range(1, n_mlp):
        att_copy(m, lax.rem(m + d, n_mlp)).wait_recv()
    attended = att_in[...].reshape(D, ROWS).T
    first = (res[...].astype(F32) + dot(attended, w_buf[...])).astype(BF16)
    first_wide = first.astype(F32)
    rows[0] = rms_scale(first_wide, gain[...])

    def rows_to(k, step, slot, slot_there, row0, count):
        return pltpu.make_async_remote_copy(
            src_ref=rows.at[slot, pl.ds(row0, count)], dst_ref=rows.at[slot_there, pl.ds(row0, count)],
            send_sem=s_rows.at[k], recv_sem=r_rows.at[k], device_id={"mlp": y_at(step)}, device_id_type=MESH,
        )

    rows_next = [rows_to(0, 1, 0, 1, 0, ROWS), rows_to(1, -1, 0, 2, 0, ROWS)]
    rows_far = [rows_to(2, 1, 1, 3, 0, HALF), rows_to(3, -1, 2, 3, HALF, HALF)]
    for copy in rows_next:
        copy.start()

    for got_it, on, to_pair in ((z_rest[0], z_far[0], pair[5]), (z_rest[1], z_far[1], pair[6])):
        got_it.wait_recv()
        on.start()
        to_pair.start()
    for got_it, on, to_pair in ((x_next_in[0], x_far[0], pair[1]), (x_next_in[1], x_far[1], pair[2])):
        got_it.wait_recv()
        on.start()
        to_pair.start()
    for got_it, on in zip(rows_next, rows_far):
        got_it.wait_recv()
        on.start()
    weights_to(9, "req", x_at(1), away, away, far_rows, XROWS, 0, XMID).wait_recv()
    pair[3].start()
    weights_to(10, "req", x_at(-1), away, away, far_rows, XROWS, XMID, LANES - XMID).wait_recv()
    pair[4].start()
    weights_to(5, "mlp", z_at(1), three, three, ZROW, ZMID - ZROW).wait_recv()
    pair[7].start()
    weights_to(6, "mlp", z_at(-1), three, three, ZMID, HID - ZMID).wait_recv()
    pair[8].start()
    for copy in rows_far:
        copy.wait_recv()
    for copy in pair:
        copy.wait_recv()

    def flat(which, c, size):
        pieces = []
        while size:
            slot, row = divmod(c, HID)
            count = min(size, HID - row)
            pieces.append(ffn[which, slot, row : row + count])
            c, size = c + count, size - count
        return pieces[0] if len(pieces) == 1 else jnp.concatenate(pieces, axis=0)

    def feed_forward(block):
        total = None
        for c in range(0, 4 * HID, CHUNK):
            size = min(CHUNK, 4 * HID - c)
            gate = dot_t(block, flat(0, c, size))
            up = dot_t(block, flat(1, c, size))
            hidden = (gate * jax.nn.sigmoid(gate) * up).astype(BF16)
            piece = dot(hidden, flat(2, c, size))
            total = piece if total is None else total + piece
        return total

    def part_to(k, step, src, dst):
        return pltpu.make_async_remote_copy(
            src_ref=src, dst_ref=dst, send_sem=s_part.at[k], recv_sem=r_part.at[k],
            device_id={"mlp": y_at(step)}, device_id_type=MESH,
        )

    part[0] = feed_forward(rows[3]).astype(BF16)
    far = [
        part_to(0, 1, part.at[0, pl.ds(0, HALF)], via.at[0]),
        part_to(1, -1, part.at[0, pl.ds(HALF, HALF)], via.at[1]),
    ]
    for copy in far:
        copy.start()
    both = feed_forward(rows[1:3].reshape(2 * ROWS, D))
    near = [part_to(2, 1, part.at[2], back.at[0]), part_to(3, -1, part.at[1], back.at[1])]
    far[0].wait_recv()
    part[2, 0:HALF] = (both[ROWS : ROWS + HALF] + via[0].astype(F32)).astype(BF16)
    part[2, HALF:] = both[ROWS + HALF :].astype(BF16)
    near[0].start()
    far[1].wait_recv()
    part[1, 0:HALF] = both[0:HALF].astype(BF16)
    part[1, HALF:] = (both[HALF:ROWS] + via[1].astype(F32)).astype(BF16)
    near[1].start()
    total = feed_forward(rows[0])
    for copy in near:
        copy.wait_recv()
    total = total + back[0].astype(F32) + back[1].astype(F32)
    second = (first_wide + total).astype(BF16)
    hidden_out[...] = second
    normed = rms_scale(second.astype(F32), next_gain[...])
    qkv_copy.wait()
    qkv_out[...] = dot(normed, qkv_buf[...]).astype(BF16)

    for d in range(1, n_mlp):
        att_copy(lax.rem(m + d, n_mlp), m).wait_send()
    for copy in z_quarter + z_rest + z_far + x_next + x_far + pair + rows_next + rows_far + far + near:
        copy.wait_send()


def layer(
    lengths, old_flags, owner, res, q, k, v, conv_w, pstate, pnorm, w_out, gain,
    w_gate, w_up, w_down, next_gain, w_qkv,
):
    smem = pl.BlockSpec(memory_space=pltpu.SMEM)
    vmem = pl.BlockSpec(memory_space=pltpu.VMEM)
    hbm = pl.BlockSpec(memory_space=pl.ANY)
    return pl.pallas_call(
        layer_kernel,
        out_shape=(jax.ShapeDtypeStruct((ROWS, D), BF16), jax.ShapeDtypeStruct((ROWS, QKV), BF16)),
        in_specs=[smem] * 3 + [vmem] * 5 + [hbm, vmem, hbm, vmem, hbm, hbm, hbm, vmem, hbm],
        out_specs=(vmem, vmem),
        scratch_shapes=[
            pltpu.VMEM((H, PACK, ROWS), BF16),
            pltpu.VMEM((H, PACK, ROWS), BF16),
            pltpu.VMEM((8, SROWS, ROWS), BF16),
            pltpu.VMEM((SEQ, FD), BF16),
            pltpu.VMEM((FD, SEQ), BF16),
            pltpu.VMEM((HD, SEQ), BF16),
            pltpu.VMEM((SROWS, SEQ), BF16),
            pltpu.VMEM((H, HD, ROWS), BF16),
            pltpu.VMEM((H, HD, ROWS), BF16),
            pltpu.VMEM((D, D), BF16),
            pltpu.VMEM((H, HD, 8), F32),
            pltpu.VMEM((1 + FD + SQ, HD), F32),
            pltpu.VMEM((3, 4, HID, D), BF16),
            pltpu.VMEM((D, QKV), BF16),
            pltpu.VMEM((4, ROWS, D), BF16),
            pltpu.VMEM((3, ROWS, D), BF16),
            pltpu.VMEM((2, HALF, D), BF16),
            pltpu.VMEM((2, ROWS, D), BF16),
            pltpu.SemaphoreType.DMA((H,)),
            pltpu.SemaphoreType.DMA((H,)),
            pltpu.SemaphoreType.DMA((8,)),
            pltpu.SemaphoreType.DMA((8,)),
            pltpu.SemaphoreType.DMA((H,)),
            pltpu.SemaphoreType.DMA((H,)),
            pltpu.SemaphoreType.DMA((6,)),
            pltpu.SemaphoreType.DMA((20,)),
            pltpu.SemaphoreType.DMA((20,)),
            pltpu.SemaphoreType.DMA((4,)),
            pltpu.SemaphoreType.DMA((4,)),
            pltpu.SemaphoreType.DMA((4,)),
            pltpu.SemaphoreType.DMA((4,)),
        ],
        compiler_params=pltpu.CompilerParams(
            collective_id=0, has_side_effects=True, vmem_limit_bytes=56 << 20
        ),
        name="layer",
    )(
        lengths, old_flags, owner, res, q, k, v, conv_w, pstate, pnorm, w_out, gain,
        w_gate, w_up, w_down, next_gain, w_qkv,
    )


def shards(
    residual_in, query_in, key_in, values_in, conv_weight, prefix_state, prefix_norm, prefix_owner,
    lengths, old_flags, out_weight, mlp_gain, gate_weight, up_weight, down_weight, next_gain, qkv_weight,
):
    return layer(
        lengths, old_flags, prefix_owner, residual_in, query_in, key_in, values_in, conv_weight,
        jnp.transpose(prefix_state, (0, 2, 1, 3)).reshape(1 + FD + SQ, 1, HD),
        prefix_norm.reshape(1, 1 + FD + SQ), out_weight, mlp_gain,
        gate_weight.T, up_weight.T, down_weight, next_gain, qkv_weight,
    )


def solution(mesh):
    placed = (
        P(("req", "mlp"), None), P(("req", "mlp"), None), P(("req", "mlp"), None), P(("req", "mlp"), None),
        P(), P("req", "mlp", None, None), P("req", "mlp", None), P(), P("req", None), P("req", None),
        P(), P(), P(None, "mlp"), P(None, "mlp"), P("mlp", None), P(), P(),
    )
    return jax.shard_map(
        shards,
        mesh=mesh,
        in_specs=placed,
        out_specs=(P(("req", "mlp"), None), P(("req", "mlp"), None)),
        check_vma=False,
    )
```

```python
import functools

import jax
import jax.numpy as jnp
from jax import lax
from jax.experimental import pallas as pl
from jax.experimental.pallas import tpu as pltpu
from jax.sharding import PartitionSpec as P

EPSILON = 1e-05
MESH = pl.DeviceIdType.MESH
F32 = jnp.float32
BF16 = jnp.bfloat16

D = 1792
H = 16
FD = 16
HD = 112
SQ = FD * FD
ROWS = 128
SEQ = 2048
PACK = 2 * FD + HD
SROWS = 288
BLK = 256
NBLK = SEQ // BLK
SPAN = 5
QKV = 2304
HID = 304
LANES = D // 2
XROWS = 48
ZROW = 4 * XROWS
ZMID = 256
XMID = 512
HALF = ROWS // 2
CHUNK = 256
EARLY_Z = True
FORWARD_AT = 3


def tdot(a, b):
    return lax.dot_general(a, b, (((0,), (0,)), ((), ())), preferred_element_type=F32)


def dot(a, b):
    return jnp.dot(a, b, preferred_element_type=F32)


def dot_t(a, b):
    return lax.dot_general(a, b, (((1,), (1,)), ((), ())), preferred_element_type=F32)


def rms_scale(wide, gain):
    return (wide * lax.rsqrt(jnp.mean(wide * wide, axis=-1, keepdims=True) + EPSILON) * gain).astype(BF16)


def layer_kernel(
    lens, flags, owner, res, q_in, k_in, v_in, conv_w, pstate, pnorm, w_out, gain,
    w_gate, w_up, w_down, next_gain, w_qkv,
    hidden_out, qkv_out,
    pack, got, states, keys, queries, values, feats, attn, att_in, w_buf, taps, state_in,
    ffn, qkv_buf, rows, part, via, back,
    s_pack, r_pack, s_state, r_state, s_att, r_att, l_sem, s_w, r_w, s_rows, r_rows, s_part, r_part,
):
    g = lax.axis_index("req")
    m = lax.axis_index("mlp")
    n_req = lax.axis_size("req")
    n_mlp = lax.axis_size("mlp")
    x, core = g // 2, lax.rem(g, 2)
    z, y = m // 4, lax.rem(m, 4)

    barrier = pltpu.get_barrier_semaphore()
    for d in range(1, n_mlp):
        pl.semaphore_signal(
            barrier, inc=1, device_id={"mlp": lax.rem(m + d, n_mlp)}, device_id_type=MESH
        )
    for d in range(1, n_req):
        pl.semaphore_signal(
            barrier, inc=1, device_id={"req": lax.rem(g + d, n_req)}, device_id_type=MESH
        )
    state_load = pltpu.make_async_copy(pstate.at[:, 0, :], state_in, l_sem.at[0])
    state_load.start()
    ffn_loads = [
        pltpu.make_async_copy(ref, ffn.at[i, 0], l_sem.at[1 + i])
        for i, ref in enumerate((w_gate, w_up, w_down))
    ]
    for load in ffn_loads:
        load.start()
    w_copy = pltpu.make_async_copy(w_out, w_buf, l_sem.at[4])
    w_copy.start()
    qkv_copy = pltpu.make_async_copy(w_qkv, qkv_buf, l_sem.at[5])
    qkv_copy.start()

    lane0 = pl.multiple_of(core * LANES, 128)

    def weights_to(k, axis, to, slots, slots_there, row0, count, lane_at=0, lane_count=LANES):
        lanes = pl.ds(pl.multiple_of(lane0 + lane_at, 128), lane_count)
        at = pl.ds(row0, count)
        return pltpu.make_async_remote_copy(
            src_ref=ffn.at[:, slots, at, lanes], dst_ref=ffn.at[:, slots_there, at, lanes],
            send_sem=s_w.at[k], recv_sem=r_w.at[k], device_id={axis: to}, device_id_type=MESH,
        )

    def z_at(step):
        return lax.rem(z + step + 4, 4) * 4 + y

    def x_at(step):
        return lax.rem(x + step + 4, 4) * 2 + core

    def y_at(step):
        return z * 4 + lax.rem(y + step + 4, 4)

    sibling = x * 2 + 1 - core
    away = pl.ds(1, 3)
    mine = pl.multiple_of(x * XROWS, 16)
    left_rows = pl.multiple_of(lax.rem(x + 3, 4) * XROWS, 16)
    right_rows = pl.multiple_of(lax.rem(x + 1, 4) * XROWS, 16)
    far_rows = pl.multiple_of(lax.rem(x + 2, 4) * XROWS, 16)
    one, two, three = pl.ds(1, 1), pl.ds(2, 1), pl.ds(3, 1)
    own = pl.ds(0, 1)
    z_quarter = [
        weights_to(0, "mlp", z_at(1), own, one, mine, XROWS),
        weights_to(1, "mlp", z_at(-1), own, two, mine, XROWS),
        weights_to(2, "mlp", z_at(2), own, three, mine, XROWS),
    ]
    z_rest = [
        weights_to(3, "mlp", z_at(1), own, one, ZROW, HID - ZROW),
        weights_to(4, "mlp", z_at(-1), own, two, ZROW, HID - ZROW),
    ]
    z_far = [
        weights_to(5, "mlp", z_at(1), one, three, ZROW, ZMID - ZROW),
        weights_to(6, "mlp", z_at(-1), two, three, ZMID, HID - ZMID),
    ]
    x_next = [
        weights_to(7, "req", x_at(1), away, away, mine, XROWS),
        weights_to(8, "req", x_at(-1), away, away, mine, XROWS),
    ]
    x_next_in = [
        weights_to(7, "req", x_at(1), away, away, left_rows, XROWS),
        weights_to(8, "req", x_at(-1), away, away, right_rows, XROWS),
    ]
    x_far = [
        weights_to(9, "req", x_at(1), away, away, left_rows, XROWS, 0, XMID),
        weights_to(10, "req", x_at(-1), away, away, right_rows, XROWS, XMID, LANES - XMID),
    ]
    pair = [
        weights_to(11, "req", sibling, away, away, mine, XROWS),
        weights_to(12, "req", sibling, away, away, left_rows, XROWS),
        weights_to(13, "req", sibling, away, away, right_rows, XROWS),
        weights_to(14, "req", sibling, away, away, far_rows, XROWS, 0, XMID),
        weights_to(15, "req", sibling, away, away, far_rows, XROWS, XMID, LANES - XMID),
        weights_to(16, "req", sibling, one, one, ZROW, HID - ZROW),
        weights_to(17, "req", sibling, two, two, ZROW, HID - ZROW),
        weights_to(18, "req", sibling, three, three, ZROW, ZMID - ZROW),
        weights_to(19, "req", sibling, three, three, ZMID, HID - ZMID),
    ]

    pack[:, 0:FD, :] = (q_in[...].T).reshape(H, FD, ROWS)
    pack[:, FD : 2 * FD, :] = (k_in[...].T).reshape(H, FD, ROWS)
    pack[:, 2 * FD :, :] = (v_in[...].T).reshape(H, HD, ROWS)

    eye = (
        lax.broadcasted_iota(jnp.int32, (1 + FD + SQ, 1 + FD + SQ), 0)
        == lax.broadcasted_iota(jnp.int32, (1 + FD + SQ, 1 + FD + SQ), 1)
    )
    norm_col = jnp.sum(jnp.where(eye, pnorm[...], 0.0), axis=1, keepdims=True)
    norm_hi = norm_col.astype(BF16).astype(F32)
    state_load.wait()
    full = jnp.concatenate(
        [
            state_in[...],
            norm_hi,
            norm_col - norm_hi,
            jnp.zeros((1 + FD + SQ, ROWS - HD - 2), F32),
        ],
        axis=1,
    )
    states[g] = jnp.concatenate(
        [
            full[1 + FD :],
            full[1 : 1 + FD],
            full[0:1],
            jnp.zeros((SROWS - 1 - FD - SQ, ROWS), F32),
        ],
        axis=0,
    ).astype(BF16)

    taps[...] = (
        jnp.concatenate([conv_w[...], jnp.zeros((5, D), F32)], axis=0).T
    ).reshape(H, HD, 8)

    pl.semaphore_wait(barrier, n_mlp - 1 + n_req - 1)

    def pack_copy(to, frm):
        return pltpu.make_async_remote_copy(
            src_ref=pack.at[to], dst_ref=got.at[frm], send_sem=s_pack.at[to], recv_sem=r_pack.at[frm],
            device_id={"mlp": to}, device_id_type=MESH,
        )

    def state_copy(to, frm):
        return pltpu.make_async_remote_copy(
            src_ref=states.at[g], dst_ref=states.at[frm], send_sem=s_state.at[to], recv_sem=r_state.at[frm],
            device_id={"req": to}, device_id_type=MESH,
        )

    for d in range(1, n_mlp):
        pack_copy(lax.rem(m + d, n_mlp), m).start()
    for d in range(1, n_req):
        state_copy(lax.rem(g + d, n_req), g).start()
    got[m] = pack[m]
    for load in ffn_loads:
        load.wait()
    for copy in z_quarter:
        copy.start()
    if EARLY_Z:
        for copy in z_rest:
            copy.start()

    b0 = lens[0, 0]
    b1 = b0 + lens[0, 1]
    b2 = b1 + lens[0, 2]
    f0, f1, f2, f3 = (flags[0, i].astype(F32) for i in range(4))

    def starts(pos):
        return jnp.where(pos >= b2, b2, jnp.where(pos >= b1, b1, jnp.where(pos >= b0, b0, 0)))

    for d in range(1, n_mlp):
        pack_copy(m, lax.rem(m + d, n_mlp)).wait_recv()
    unit = (lax.broadcasted_iota(jnp.int32, (FD, ROWS), 0) == 0).astype(F32).astype(BF16)
    for j in range(H):
        at = slice(j * ROWS, (j + 1) * ROWS)
        queries[0:FD, at] = (got[j, 0:FD, :].astype(F32) * 0.25).astype(BF16)
        queries[FD:, at] = unit
        keys[at, :] = jnp.concatenate([got[j, FD : 2 * FD, :], unit], axis=0).T
        values[HD:, at] = unit
    raw = jnp.concatenate([got[j, 2 * FD :, :] for j in range(H)], axis=1).astype(F32)
    pos = lax.broadcasted_iota(jnp.int32, (1, SEQ), 1)
    start = starts(pos)
    tap_cols = taps[m]
    conv = tap_cols[:, 0:1] * raw
    for tap in (1, 2):
        conv = conv + tap_cols[:, tap : tap + 1] * jnp.where(pos - tap >= start, pltpu.roll(raw, tap, 1), 0.0)
    values[0:HD, :] = conv.astype(BF16)

    old = jnp.where(pos >= b2, f3, jnp.where(pos >= b1, f2, jnp.where(pos >= b0, f1, f0)))
    qf = queries[0:FD, :].astype(F32)
    for a in range(FD):
        feats[a * FD : (a + 1) * FD, :] = (
            old * (qf[a : a + 1] * qf * (32.0 / 32.0**0.5))
        ).astype(BF16)
    feats[SQ : SQ + FD, :] = (old * (4.0 * qf)).astype(BF16)
    feats[SQ + FD :, :] = jnp.concatenate([2.0 * old, jnp.zeros((SROWS - SQ - FD - 1, SEQ), F32)], axis=0).astype(BF16)

    for d in range(1, n_req):
        state_copy(g, lax.rem(g + d, n_req)).wait_recv()
    own_state = states[owner[g]].T

    def att_copy(to, frm):
        return pltpu.make_async_remote_copy(
            src_ref=attn.at[to], dst_ref=att_in.at[frm], send_sem=s_att.at[to], recv_sem=r_att.at[frm],
            device_id={"mlp": to}, device_id_type=MESH,
        )

    def query_block(i):
        at = slice(i * BLK, (i + 1) * BLK)
        q_pos = i * BLK + lax.broadcasted_iota(jnp.int32, (1, BLK), 1)
        q_start = starts(q_pos)
        first_key = max(0, i - (SPAN - 1))
        scores = []
        for j in range(first_key, i + 1):
            root = dot(keys[j * BLK : (j + 1) * BLK, :], queries[:, at])
            k_pos = j * BLK + lax.broadcasted_iota(jnp.int32, (BLK, 1), 0)
            seen = k_pos >= q_start
            if j == i:
                seen = seen & (k_pos <= q_pos)
            scores.append(jnp.where(seen, root * root + 1.0, 0.0).astype(BF16))
        sums = dot(own_state, feats[:, at])
        den_old = sums[HD : HD + 1] + sums[HD + 1 : HD + 2]
        new = dot(values[:, first_key * BLK : (i + 1) * BLK], jnp.concatenate(scores, axis=0))
        out = ((sums[:HD] + new[:HD]) / (den_old + new[HD : HD + 1])).astype(BF16)
        for half in range(BLK // ROWS):
            to = i * (BLK // ROWS) + half
            attn[to] = out[:, half * ROWS : (half + 1) * ROWS]

            @pl.when(to != m)
            def _():
                att_copy(to, m).start()

            @pl.when(to == m)
            def _():
                att_in[m] = out[:, half * ROWS : (half + 1) * ROWS]

    for i in range(NBLK):
        query_block(i)
        if i == FORWARD_AT:
            for copy in z_quarter:
                copy.wait_recv()
            for copy in x_next:
                copy.start()
            pair[0].start()

    if not EARLY_Z:
        for copy in z_rest:
            copy.start()
    for d in range(1, n_mlp):
        pack_copy(lax.rem(m + d, n_mlp), m).wait_send()
    for d in range(1, n_req):
        state_copy(lax.rem(g + d, n_req), g).wait_send()
    w_copy.wait()
    for d in range(1, n_mlp):
        att_copy(m, lax.rem(m + d, n_mlp)).wait_recv()
    attended = att_in[...].reshape(D, ROWS).T
    first = (res[...].astype(F32) + dot(attended, w_buf[...])).astype(BF16)
    first_wide = first.astype(F32)
    rows[0] = rms_scale(first_wide, gain[...])

    def rows_to(k, step, slot, slot_there, row0, count):
        return pltpu.make_async_remote_copy(
            src_ref=rows.at[slot, pl.ds(row0, count)], dst_ref=rows.at[slot_there, pl.ds(row0, count)],
            send_sem=s_rows.at[k], recv_sem=r_rows.at[k], device_id={"mlp": y_at(step)}, device_id_type=MESH,
        )

    rows_next = [rows_to(0, 1, 0, 1, 0, ROWS), rows_to(1, -1, 0, 2, 0, ROWS)]
    rows_far = [rows_to(2, 1, 1, 3, 0, HALF), rows_to(3, -1, 2, 3, HALF, HALF)]
    for copy in rows_next:
        copy.start()

    for got_it, on, to_pair in ((x_next_in[0], x_far[0], pair[1]), (x_next_in[1], x_far[1], pair[2])):
        got_it.wait_recv()
        on.start()
        to_pair.start()
    for got_it, on, to_pair in ((z_rest[0], z_far[0], pair[5]), (z_rest[1], z_far[1], pair[6])):
        got_it.wait_recv()
        on.start()
        to_pair.start()
    for got_it, on in zip(rows_next, rows_far):
        got_it.wait_recv()
        on.start()
    weights_to(9, "req", x_at(1), away, away, far_rows, XROWS, 0, XMID).wait_recv()
    pair[3].start()
    weights_to(10, "req", x_at(-1), away, away, far_rows, XROWS, XMID, LANES - XMID).wait_recv()
    pair[4].start()
    weights_to(5, "mlp", z_at(1), three, three, ZROW, ZMID - ZROW).wait_recv()
    pair[7].start()
    weights_to(6, "mlp", z_at(-1), three, three, ZMID, HID - ZMID).wait_recv()
    pair[8].start()
    for copy in rows_far:
        copy.wait_recv()
    for copy in pair:
        copy.wait_recv()

    def flat(which, c, size):
        pieces = []
        while size:
            slot, row = divmod(c, HID)
            count = min(size, HID - row)
            pieces.append(ffn[which, slot, row : row + count])
            c, size = c + count, size - count
        return pieces[0] if len(pieces) == 1 else jnp.concatenate(pieces, axis=0)

    def feed_forward(block):
        total = None
        for c in range(0, 4 * HID, CHUNK):
            size = min(CHUNK, 4 * HID - c)
            gate = dot_t(block, flat(0, c, size))
            up = dot_t(block, flat(1, c, size))
            hidden = (gate * jax.nn.sigmoid(gate) * up).astype(BF16)
            piece = dot(hidden, flat(2, c, size))
            total = piece if total is None else total + piece
        return total

    def part_to(k, step, src, dst):
        return pltpu.make_async_remote_copy(
            src_ref=src, dst_ref=dst, send_sem=s_part.at[k], recv_sem=r_part.at[k],
            device_id={"mlp": y_at(step)}, device_id_type=MESH,
        )

    part[0] = feed_forward(rows[3]).astype(BF16)
    far = [
        part_to(0, 1, part.at[0, pl.ds(0, HALF)], via.at[0]),
        part_to(1, -1, part.at[0, pl.ds(HALF, HALF)], via.at[1]),
    ]
    for copy in far:
        copy.start()
    both = feed_forward(rows[1:3].reshape(2 * ROWS, D))
    near = [part_to(2, 1, part.at[2], back.at[0]), part_to(3, -1, part.at[1], back.at[1])]
    far[0].wait_recv()
    part[2, 0:HALF] = (both[ROWS : ROWS + HALF] + via[0].astype(F32)).astype(BF16)
    part[2, HALF:] = both[ROWS + HALF :].astype(BF16)
    near[0].start()
    far[1].wait_recv()
    part[1, 0:HALF] = both[0:HALF].astype(BF16)
    part[1, HALF:] = (both[HALF:ROWS] + via[1].astype(F32)).astype(BF16)
    near[1].start()
    total = feed_forward(rows[0])
    for copy in near:
        copy.wait_recv()
    total = total + back[0].astype(F32) + back[1].astype(F32)
    second = (first_wide + total).astype(BF16)
    hidden_out[...] = second
    normed = rms_scale(second.astype(F32), next_gain[...])
    qkv_copy.wait()
    qkv_out[...] = dot(normed, qkv_buf[...]).astype(BF16)

    for d in range(1, n_mlp):
        att_copy(lax.rem(m + d, n_mlp), m).wait_send()
    for copy in z_quarter + z_rest + z_far + x_next + x_far + pair + rows_next + rows_far + far + near:
        copy.wait_send()


def layer(
    lengths, old_flags, owner, res, q, k, v, conv_w, pstate, pnorm, w_out, gain,
    w_gate, w_up, w_down, next_gain, w_qkv,
):
    smem = pl.BlockSpec(memory_space=pltpu.SMEM)
    vmem = pl.BlockSpec(memory_space=pltpu.VMEM)
    hbm = pl.BlockSpec(memory_space=pl.ANY)
    return pl.pallas_call(
        layer_kernel,
        out_shape=(jax.ShapeDtypeStruct((ROWS, D), BF16), jax.ShapeDtypeStruct((ROWS, QKV), BF16)),
        in_specs=[smem] * 3 + [vmem] * 5 + [hbm, vmem, hbm, vmem, hbm, hbm, hbm, vmem, hbm],
        out_specs=(vmem, vmem),
        scratch_shapes=[
            pltpu.VMEM((H, PACK, ROWS), BF16),
            pltpu.VMEM((H, PACK, ROWS), BF16),
            pltpu.VMEM((8, SROWS, ROWS), BF16),
            pltpu.VMEM((SEQ, 2 * FD), BF16),
            pltpu.VMEM((2 * FD, SEQ), BF16),
            pltpu.VMEM((HD + FD, SEQ), BF16),
            pltpu.VMEM((SROWS, SEQ), BF16),
            pltpu.VMEM((H, HD, ROWS), BF16),
            pltpu.VMEM((H, HD, ROWS), BF16),
            pltpu.VMEM((D, D), BF16),
            pltpu.VMEM((H, HD, 8), F32),
            pltpu.VMEM((1 + FD + SQ, HD), F32),
            pltpu.VMEM((3, 4, HID, D), BF16),
            pltpu.VMEM((D, QKV), BF16),
            pltpu.VMEM((4, ROWS, D), BF16),
            pltpu.VMEM((3, ROWS, D), BF16),
            pltpu.VMEM((2, HALF, D), BF16),
            pltpu.VMEM((2, ROWS, D), BF16),
            pltpu.SemaphoreType.DMA((H,)),
            pltpu.SemaphoreType.DMA((H,)),
            pltpu.SemaphoreType.DMA((8,)),
            pltpu.SemaphoreType.DMA((8,)),
            pltpu.SemaphoreType.DMA((H,)),
            pltpu.SemaphoreType.DMA((H,)),
            pltpu.SemaphoreType.DMA((6,)),
            pltpu.SemaphoreType.DMA((20,)),
            pltpu.SemaphoreType.DMA((20,)),
            pltpu.SemaphoreType.DMA((4,)),
            pltpu.SemaphoreType.DMA((4,)),
            pltpu.SemaphoreType.DMA((4,)),
            pltpu.SemaphoreType.DMA((4,)),
        ],
        compiler_params=pltpu.CompilerParams(
            collective_id=0, has_side_effects=True, vmem_limit_bytes=56 << 20
        ),
        name="layer",
    )(
        lengths, old_flags, owner, res, q, k, v, conv_w, pstate, pnorm, w_out, gain,
        w_gate, w_up, w_down, next_gain, w_qkv,
    )


def shards(
    residual_in, query_in, key_in, values_in, conv_weight, prefix_state, prefix_norm, prefix_owner,
    lengths, old_flags, out_weight, mlp_gain, gate_weight, up_weight, down_weight, next_gain, qkv_weight,
):
    return layer(
        lengths, old_flags, prefix_owner, residual_in, query_in, key_in, values_in, conv_weight,
        jnp.transpose(prefix_state, (0, 2, 1, 3)).reshape(1 + FD + SQ, 1, HD),
        prefix_norm.reshape(1, 1 + FD + SQ), out_weight, mlp_gain,
        gate_weight.T, up_weight.T, down_weight, next_gain, qkv_weight,
    )


def solution(mesh):
    placed = (
        P(("req", "mlp"), None), P(("req", "mlp"), None), P(("req", "mlp"), None), P(("req", "mlp"), None),
        P(), P("req", "mlp", None, None), P("req", "mlp", None), P(), P("req", None), P("req", None),
        P(), P(), P(None, "mlp"), P(None, "mlp"), P("mlp", None), P(), P(),
    )
    return jax.shard_map(
        shards,
        mesh=mesh,
        in_specs=placed,
        out_specs=(P(("req", "mlp"), None), P(("req", "mlp"), None)),
        check_vma=False,
    )
```
